32 devices in a mesh: dp: 4 (over y, x), region: 8 (over z, core).
Axes of the slice: x: 2, y: 2, z: 4, core: 2. Of those that a mesh axis runs over, the one named last changes fastest.
Arguments:
- features: bfloat16 [4, 8, 16, 16, 16, 128], P('dp', 'region'), may hold values from -6 to 6
- conv_weight: bfloat16 [3, 3, 3, 128, 128], replicated, may hold values from -0.109375 to 0.109375
- down_weight: bfloat16 [2, 2, 2, 128, 128], replicated, may hold values from -0.1875 to 0.1875
- coarse_cotangent: bfloat16 [4, 8, 16, 16, 16, 128], P('dp', 'region'), may hold values from -6 to 6
- brick_coords: int32 [4, 8, 3], P('dp', 'region'), may hold values from 0 to 7, as said below
- neighbours: int32 [4, 8, 26], P('dp', 'region'), may hold values from -1 to 7, as said below
- parents: int32 [4, 8], P('dp', 'region'), may hold values from 0 to 7, as said below
Outputs:
- coarse_features: bfloat16 [4, 8, 16, 16, 16, 128], P('dp', 'region')
- input_grad: bfloat16 [4, 8, 16, 16, 16, 128], P('dp', 'region')
- conv_grad: float32 [3, 3, 3, 128, 128], replicated
- down_grad: float32 [2, 2, 2, 128, 128], replicated
The draws below stay inside these ranges and needn't reach their ends.
Inputs may be any that keep to these rules, and one draw needn't show every extreme that they name: `brick_coords`: slot s lies on region index s; its first coordinate is s, the second below 4, the third below 2; the coordinates of one scene's slots are distinct. `neighbours`: entry d names the slot whose coordinates are the brick's own plus offset d, or -1 where no slot has them; named slots lie on the same or an adjacent region index, and the relation is symmetric. `parents`: the parent is 2 (x // 2) + (y // 2) of the brick's coordinates; coarse brick c lies on region index c.
All inputs are finite; a program needn't handle non-finite values.
Results may differ from the reference program's by a relative error of at most 0.005.
Values may be sent and summed in bfloat16 or wider, within the bound.
A program may use at most 192 MiB of HBM per device.

```python
import jax
import jax.numpy as jnp
import numpy as np
from jax import lax

CHANNELS = 128
BRICK = 16
BRICK_DEV = 1
GRID_Y = 4
GRID_Z = 2
SCENES = 4
TOTAL_BRICKS = 8
COARSE = 8
N_REGION = 8


OFFSET_TABLE = np.array([(a, b, c) for a in (-1, 0, 1) for b in (-1, 0, 1) for c in (-1, 0, 1) if (a, b, c) != (0, 0, 0)], dtype=np.int32)


def brick_layout(key):
    keys = jax.random.split(jax.random.fold_in(key, 7), SCENES * N_REGION)
    places = jax.vmap(lambda single: jax.random.permutation(single, GRID_Y * GRID_Z))(keys)[:, :BRICK_DEV]
    places = places.reshape(SCENES, TOTAL_BRICKS).astype(jnp.int32)
    first = jnp.broadcast_to((jnp.arange(TOTAL_BRICKS, dtype=jnp.int32) // BRICK_DEV)[None, :], (SCENES, TOTAL_BRICKS))
    return jnp.stack([first, places // GRID_Z, places % GRID_Z], axis=-1).astype(jnp.int32)


def draw_brick_coords(key, part):
    return brick_layout(key)


def draw_neighbours(key, part):
    coords = brick_layout(key)
    wanted = coords[:, :, None, :] + jnp.asarray(OFFSET_TABLE)[None, None, :, :]
    matches = jnp.all(wanted[:, :, :, None, :] == coords[:, None, None, :, :], axis=-1).astype(jnp.int32)
    labels = jnp.arange(1, TOTAL_BRICKS + 1, dtype=jnp.int32)
    return (jnp.sum(matches * labels, axis=-1) - 1).astype(jnp.int32)


def draw_parents(key, part):
    coords = brick_layout(key)
    return (2 * (coords[:, :, 0] // 2) + coords[:, :, 1] // 2).astype(jnp.int32)


def block_levels(key, extent, cuts, least, high):
    factor_of, own = 1.0, jax.random.fold_in(key, 6)
    for position, shards_of in cuts:
        heights = jnp.exp(jax.random.uniform(jax.random.fold_in(own, position), (shards_of,), jnp.float32, least / len(cuts), high / len(cuts)))
        factor_of = factor_of * jnp.repeat(heights, extent[position] // shards_of).reshape([-1 if axis == position else 1 for axis in range(len(extent))])
    return factor_of


def centred(own_key, shape, deviation, reach, cuts=(), held_as=jnp.bfloat16):
    values = jax.random.normal(own_key, shape, jnp.float32) * deviation
    if len(cuts) > 0:
        values = block_levels(own_key, shape, cuts, -0.22, 0.18) * values
    return jnp.clip(values, min=-reach, max=reach).astype(held_as)


def setup_inputs(seed: int = 0) -> dict:
    key_of = jax.random.split(jax.random.key(seed), 8)
    return {
        "features": centred(key_of[0], (SCENES, TOTAL_BRICKS, BRICK, BRICK, BRICK, CHANNELS), 1.0, 6.0, ((0, 4), (1, 8))),
        "conv_weight": centred(key_of[1], (3, 3, 3, CHANNELS, CHANNELS), (27 * CHANNELS) ** -0.5, 0.109375),
        "down_weight": centred(key_of[2], (2, 2, 2, CHANNELS, CHANNELS), (8 * CHANNELS) ** -0.5, 0.1875),
        "coarse_cotangent": centred(key_of[3], (SCENES, COARSE, BRICK, BRICK, BRICK, CHANNELS), 1.0, 6.0, ((0, 4), (1, 8))),
        "brick_coords": draw_brick_coords(jax.random.fold_in(key_of[7], 71), 0),
        "neighbours": draw_neighbours(jax.random.fold_in(key_of[7], 71), 0),
        "parents": draw_parents(jax.random.fold_in(key_of[7], 71), 0),
    }


OFFSETS = [(a, b, c) for a in (-1, 0, 1) for b in (-1, 0, 1) for c in (-1, 0, 1) if (a, b, c) != (0, 0, 0)]
loss_scale = 1024.0


def source_cut(offset, brick_edge):
    if offset < 0:
        return slice(brick_edge - 1, brick_edge)
    if offset == 0:
        return slice(0, brick_edge)
    return slice(0, 1)


def pad_bricks(center, fetcher, present):
    pieces = {}
    for number, (a, b, c) in enumerate(OFFSETS):
        section = fetcher(number, a, b, c)
        keeper = present[:, number].reshape(-1, 1, 1, 1, 1)
        pieces[(a, b, c)] = jnp.where(keeper, section, jnp.zeros_like(section))
    pieces[(0, 0, 0)] = center
    slabs = []
    for a in (-1, 0, 1):
        rows = []
        for b in (-1, 0, 1):
            rows.append(jnp.concatenate([pieces[(a, b, c)] for c in (-1, 0, 1)], axis=3))
        slabs.append(jnp.concatenate(rows, axis=2))
    return jnp.concatenate(slabs, axis=1)


def tap_windows(padded, a):
    brick_edge, channels = padded.shape[1] - 2, padded.shape[-1]
    parts = [padded[:, a:a + brick_edge, b:b + brick_edge, c:c + brick_edge] for b in range(3) for c in range(3)]
    return jnp.concatenate(parts, axis=-1).reshape(-1, 9 * channels)


def conv_bricks(padded, kernel):
    brick_count, brick_edge, channels = padded.shape[0], padded.shape[1] - 2, padded.shape[-1]
    summed = jnp.zeros((brick_count * brick_edge ** 3, kernel.shape[-1]), jnp.float32)
    for a in range(3):
        window = tap_windows(padded, a)
        summed = summed + jnp.dot(window, kernel[a].reshape(9 * channels, -1), preferred_element_type=jnp.float32)
    return summed.reshape(brick_count, brick_edge, brick_edge, brick_edge, -1)


def kernel_grads(padded, grads):
    channels = padded.shape[-1]
    flat_grads = grads.reshape(-1, grads.shape[-1])
    result = []
    for a in range(3):
        window = tap_windows(padded, a)
        result.append(lax.dot_general(window, flat_grads, (((0,), (0,)), ((), ())), preferred_element_type=jnp.float32).reshape(3, 3, channels, -1))
    return jnp.stack(result)


def padded_scene(field, neighbours):
    brick_edge = field.shape[1]
    present = neighbours >= 0
    indices = jnp.where(present, neighbours, 0).astype(jnp.int32)

    def fetcher(number, a, b, c):
        return field[:, source_cut(a, brick_edge), source_cut(b, brick_edge), source_cut(c, brick_edge)][indices[:, number]]

    return pad_bricks(field, fetcher, present)


def reference(features, conv_weight, down_weight, coarse_cotangent, brick_coords, neighbours, parents):
    brick_edge, channels = features.shape[2], features.shape[-1]
    half_edge = brick_edge // 2
    brick_count = features.shape[1]
    coarse_count = coarse_cotangent.shape[1]
    flipped = jnp.swapaxes(jnp.flip(conv_weight, (0, 1, 2)), 3, 4)
    conv_total = jnp.zeros((3, 3, 3, channels, channels), jnp.float32)
    down_total = jnp.zeros((2, 2, 2, channels, channels), jnp.float32)
    coarse_list = []
    grad_list = []
    for scene in range(features.shape[0]):
        field = features[scene]
        padded = padded_scene(field, neighbours[scene])
        outputs = (conv_bricks(padded, conv_weight) + field.astype(jnp.float32)).astype(jnp.bfloat16)
        fine_split = outputs.reshape(brick_count, half_edge, 2, half_edge, 2, half_edge, 2, channels).astype(jnp.float32)
        blocks = jnp.einsum("bixjykzc,xyzcd->bijkd", fine_split, down_weight.astype(jnp.float32)).astype(jnp.bfloat16)
        coords = brick_coords[scene]
        octant = (coords[:, 0] % 2) * 4 + (coords[:, 1] % 2) * 2 + coords[:, 2] % 2
        targets = (parents[scene] * 8 + octant).astype(jnp.int32)
        coarse = jnp.zeros((coarse_count * 8, half_edge, half_edge, half_edge, channels), jnp.float32)
        coarse = coarse.at[targets].add(blocks.astype(jnp.float32))
        coarse = coarse.reshape(coarse_count, 2, 2, 2, half_edge, half_edge, half_edge, channels)
        coarse = coarse.transpose(0, 1, 4, 2, 5, 3, 6, 7).reshape(coarse_count, brick_edge, brick_edge, brick_edge, channels)
        coarse_list.append(coarse.astype(jnp.bfloat16))
        cotangent = coarse_cotangent[scene].reshape(coarse_count, 2, half_edge, 2, half_edge, 2, half_edge, channels)
        cotangent = cotangent.transpose(0, 1, 3, 5, 2, 4, 6, 7).reshape(coarse_count * 8, half_edge, half_edge, half_edge, channels)
        chosen = cotangent[targets]
        grad_outputs = jnp.einsum("bijkd,xyzcd->bixjykzc", chosen.astype(jnp.float32), down_weight.astype(jnp.float32))
        grad_outputs = grad_outputs.reshape(brick_count, brick_edge, brick_edge, brick_edge, channels).astype(jnp.bfloat16)
        down_total = down_total + jnp.einsum("bixjykzc,bijkd->xyzcd", fine_split, chosen.astype(jnp.float32))
        padded_back = padded_scene(grad_outputs, neighbours[scene])
        input_grad = grad_outputs.astype(jnp.float32) + conv_bricks(padded_back, flipped)
        grad_list.append(input_grad.astype(jnp.bfloat16))
        conv_total = conv_total + kernel_grads(padded, grad_outputs)
    return (jnp.stack(coarse_list), jnp.stack(grad_list), conv_total / loss_scale, down_total / loss_scale)
```

```python
import functools

import jax
import jax.numpy as jnp
from jax import lax
from jax.experimental import pallas as pl
from jax.experimental.pallas import tpu as pltpu
from jax.sharding import PartitionSpec as P

loss_scale = 1024.0
MESH = pl.DeviceIdType.MESH
F32, BF16 = jnp.float32, jnp.bfloat16


def passed_along(value, axis, by):
    peers = lax.axis_size(axis)
    pairs = [(i, i + by) for i in range(peers) if 0 <= i + by < peers]
    return lax.ppermute(value, axis, pairs)


def partner(block, axis):
    count = lax.axis_size(axis)
    return lax.ppermute(block, axis, [(i, i ^ 1) for i in range(count)])


def nn(a, b):
    return lax.dot_general(a, b, (((1,), (0,)), ((), ())), preferred_element_type=F32)


def nt(a, b):
    return lax.dot_general(a, b, (((1,), (1,)), ((), ())), preferred_element_type=F32)


def shifted(s, low, mid, high):
    edge = s.shape[-2]
    axis = s.ndim - 2
    row = lax.broadcasted_iota(jnp.int32, s.shape, axis)
    first = pltpu.roll(s, 1, axis) * jnp.where(row == 0, low, mid)
    last = pltpu.roll(s, edge - 1, axis) * jnp.where(row == edge - 1, high, mid)
    return first, s * mid, last


def put_plane(dst, x, even, odd, low, mid, high):
    half, c = even.shape[0], even.shape[-1]
    for k, v in enumerate(shifted(even, low, mid, high)):
        dst[x, 0:half, :, 2 * k * c + c : 2 * k * c + 2 * c] = v.astype(BF16)
    for k, v in enumerate(shifted(odd, low, mid, high)):
        dst[x, 1 : half + 1, :, 2 * k * c : 2 * k * c + c] = v.astype(BF16)


def put_row(dst, x, y, row, low, mid, high):
    c = row.shape[-1]
    for k, v in enumerate(shifted(row, low, mid, high)):
        at = 2 * k * c + (y % 2) * c
        dst[x, y // 2, :, at : at + c] = v.astype(BF16)


def masks(nb, a):
    def m(b, c):
        i = (a + 1) * 9 + (b + 1) * 3 + (c + 1)
        i = i - 1 if i > 13 else i
        return jnp.where(nb[i] >= 0, 1.0, 0.0).astype(F32)

    return {b: (m(b, -1), m(b, 0), m(b, 1)) for b in (-1, 0, 1)}


def put_halo(dst, x, even, odd, mask):
    half, edge = even.shape[0], dst.shape[0]
    put_plane(dst, x, even, odd, *mask[0])
    put_row(dst, x, 0, odd[half - 1], *mask[-1])
    put_row(dst, x, edge - 1, even[0], *mask[1])


def zero_rows(dst, edge, c):
    z = jnp.zeros((edge, dst.shape[2], c), BF16)
    for k in range(3):
        dst[1 : edge + 1, 0, :, 2 * k * c : 2 * k * c + c] = z
        dst[1 : edge + 1, edge // 2, :, 2 * k * c + c : 2 * k * c + 2 * c] = z


def tap_of(s, pin, pout):
    b = 2 * s + pin - pout
    return b if 0 <= b <= 2 else None


def compute_kernel(
    nb, f, flo, fhi, ch, clo, chi, cw, dw, blocks, ig, acc,
    field, wide, gfold, up, outf, gt, tt,
):
    edge, c = f.shape[0], f.shape[-1]
    half = edge // 2
    rows = half * edge

    def window(x, n, a, s):
        return field[pl.ds(x + a, n), s : s + half].reshape(n * rows, 6 * c)

    def lhs(x, n):
        return jnp.concatenate([window(x, n, a, s) for a in range(3) for s in range(2)], -1)

    def lift(v, shape):
        up[...] = jnp.zeros_like(up)
        n = v.shape[0] * v.shape[1]
        v = v.astype(F32).reshape(n, half, c)
        for r in range(2):
            up[r, 0:n, pl.ds(r, half, 2), :] = v
        both = [up[r, 0:n].reshape(n * edge, c).astype(BF16) for r in range(2)]
        return jnp.concatenate(both, -1)

    def dwt(p):
        return jnp.concatenate(
            [jnp.concatenate([dw[4 * p + 2 * q + r] for r in range(2)], -1) for q in range(2)], 0
        )

    raised = lift(ch[...], None)
    for p in range(2):
        g = nt(raised, dwt(p)).astype(BF16).reshape(half, half, edge, 2 * c)
        for i in range(half):
            gfold[2 * i + p] = g[i]
    glo = nt(lift(clo[...][None], None), dwt(1)).astype(BF16).astype(F32)
    ghi = nt(lift(chi[...][None], None), dwt(0)).astype(BF16).astype(F32)
    glo = glo.reshape(half, edge, 2 * c)
    ghi = ghi.reshape(half, edge, 2 * c)

    below, above = masks(nb, -1), masks(nb, 1)
    zero_rows(field, edge, c)
    put_halo(field, 0, flo[:, 0].astype(F32), flo[:, 1].astype(F32), below)
    put_halo(field, edge + 1, fhi[:, 0].astype(F32), fhi[:, 1].astype(F32), above)

    @pl.loop(0, edge)
    def _(x):
        put_plane(field, x + 1, f[x, :, 0].astype(F32), f[x, :, 1].astype(F32), 0.0, 1.0, 0.0)

    flat = gfold[...].reshape(edge * rows, 2 * c)
    gt[...] = flat.astype(F32).T.astype(BF16)
    for a in range(3):
        for s in range(2):
            tt[s] = nn(gt[...], window(0, edge, a, s))
        for b in range(3):
            for k in range(3):
                total = jnp.zeros((c, c), F32)
                for s in range(2):
                    for pin in range(2):
                        for pout in range(2):
                            if tap_of(s, pin, pout) == b:
                                at = (2 * k + pin) * c
                                total += tt[s, pout * c : (pout + 1) * c, at : at + c]
                tap = 9 * a + 3 * b + k
                acc[tap * c : (tap + 1) * c] = total.T * (1.0 / loss_scale)

    zero = jnp.zeros((c, c), BF16)
    for a in range(3):
        for s in range(2):
            for k in range(3):
                for pin in range(2):
                    at = ((2 * a + s) * 3 + k) * 2 * c + pin * c
                    for pout in range(2):
                        b = tap_of(s, pin, pout)
                        wide[at : at + c, pout * c : (pout + 1) * c] = (
                            zero if b is None else cw[9 * a + 3 * b + k]
                        )
    step = 4

    @pl.loop(0, edge // step)
    def _(n):
        x = n * step
        out = nn(lhs(x, step), wide[...]).reshape(step, half, edge, 2 * c)
        for q in range(2):
            own = f[pl.ds(x, step), :, q].astype(F32)
            outf[q, pl.ds(x, step)] = (
                (out[..., q * c : (q + 1) * c] + own).astype(BF16).astype(F32)
            )

    taken = []
    for p in range(2):
        for r in range(2):
            halves = []
            for q in range(2):
                parts = [
                    outf[q, 2 * i + p, :, pl.ds(r, half, 2), :].reshape(half * half, c)
                    for i in range(half)
                ]
                halves.append(jnp.concatenate(parts, 0).astype(BF16))
            taken.append(jnp.concatenate(halves, -1))
    dwf = jnp.concatenate(
        [dw[4 * p + 2 * q + r] for p in range(2) for r in range(2) for q in range(2)], 0
    )
    blocks[...] = nn(jnp.concatenate(taken, -1), dwf).astype(BF16).reshape(blocks.shape)
    cht = ch[...].reshape(half**3, c).astype(F32).T.astype(BF16)
    for p in range(2):
        for r in range(2):
            d = nn(cht, taken[2 * p + r])
            for q in range(2):
                at = (27 + 4 * p + 2 * q + r) * c
                acc[at : at + c] = d[:, q * c : (q + 1) * c].T * (1.0 / loss_scale)
    rest = acc.shape[0] - 35 * c
    if rest:
        acc[35 * c :] = jnp.zeros((rest, c), F32)

    put_halo(field, 0, glo[..., :c], glo[..., c:], below)
    put_halo(field, edge + 1, ghi[..., :c], ghi[..., c:], above)

    @pl.loop(0, edge)
    def _(x):
        g = gfold[x].astype(F32)
        put_plane(field, x + 1, g[..., :c], g[..., c:], 0.0, 1.0, 0.0)

    for a in range(3):
        for s in range(2):
            for k in range(3):
                for pin in range(2):
                    for pout in range(2):
                        b = tap_of(s, pin, pout)
                        at = ((2 * a + s) * 3 + k) * 2 * c + pin * c
                        wt = zero if b is None else cw[9 * (2 - a) + 3 * (2 - b) + 2 - k]
                        wide[at : at + c, pout * c : (pout + 1) * c] = (
                            zero if b is None else wt.T
                        )

    @pl.loop(0, edge // step)
    def _(n):
        x = n * step
        out = nn(lhs(x, step), wide[...]).reshape(step, half, edge, 2 * c)
        out = (out + gfold[pl.ds(x, step)].astype(F32)).astype(BF16)
        for q in range(2):
            ig[pl.ds(x, step), :, q] = out[..., q * c : (q + 1) * c]


def compute(nb, f, flo, fhi, ch, clo, chi, cw, dw, acc_rows):
    edge, c = f.shape[0], f.shape[-1]
    half = edge // 2
    vmem = pl.BlockSpec(memory_space=pltpu.VMEM)
    return pl.pallas_call(
        compute_kernel,
        out_shape=(
            jax.ShapeDtypeStruct((half, half, half, c), BF16),
            jax.ShapeDtypeStruct((edge, half, 2, edge, c), BF16),
            jax.ShapeDtypeStruct((acc_rows, c), F32),
        ),
        in_specs=[pl.BlockSpec(memory_space=pltpu.SMEM)] + [vmem] * 8,
        out_specs=(vmem, vmem, vmem),
        scratch_shapes=[
            pltpu.VMEM((edge + 2, half + 1, edge, 6 * c), BF16),
            pltpu.VMEM((36 * c, 2 * c), BF16),
            pltpu.VMEM((edge, half, edge, 2 * c), BF16),
            pltpu.VMEM((2, half * half, edge, c), F32),
            pltpu.VMEM((2, edge, half, edge, c), F32),
            pltpu.VMEM((2 * c, edge * half * edge), BF16),
            pltpu.VMEM((2, 2 * c, 6 * c), F32),
        ],
        compiler_params=pltpu.CompilerParams(vmem_limit_bytes=60 * 1024 * 1024),
    )(nb, f.reshape(edge, half, 2, edge, c), flo.reshape(half, 2, edge, c),
      fhi.reshape(half, 2, edge, c), ch, clo, chi, cw, dw)


def reduce_kernel(
    dps, zs, acc, conv, down, from_core, half_sum, to_dp, from_dp, quarter, to_z, from_z, whole,
    s1, r1, s2, r2, s3, r3, s4, r4, s5, r5, s6, r6,
):
    dp, region = lax.axis_index("dp"), lax.axis_index("region")
    core, z = lax.rem(region, 2), lax.div(region, 2)
    total = acc.shape[0]
    h = total // 2
    q = h // dps
    s = q // zs
    mate = (dp, region + 1 - 2 * core)

    def dp_at(k):
        return lax.rem(dp + k, dps)

    def z_at(k):
        return lax.rem(z + k, zs)

    peers = [mate]
    peers += [(dp_at(k), region) for k in range(1, dps)]
    peers += [(dp, 2 * z_at(k) + core) for k in range(1, zs)]
    barrier = pltpu.get_barrier_semaphore()
    for peer in peers:
        pl.semaphore_signal(barrier, inc=1, device_id=peer, device_id_type=MESH)
    pl.semaphore_wait(barrier, len(peers))

    def send(src, dst, ss, rs, to):
        copy = pltpu.make_async_remote_copy(
            src_ref=src, dst_ref=dst, send_sem=ss, recv_sem=rs, device_id=to, device_id_type=MESH
        )
        copy.start()
        return copy

    def rows(start, n):
        return pl.ds(pl.multiple_of(start, 16), n)

    copy = send(acc.at[rows((1 - core) * h, h)], from_core, s1.at[0], r1.at[0], mate)
    copy.wait()
    half_sum[...] = acc[rows(core * h, h)] + from_core[...]
    to_dp[...] = half_sum[...].astype(BF16)
    copies = [
        send(to_dp.at[rows(dp_at(k) * q, q)], from_dp.at[k - 1], s2.at[k - 1], r2.at[k - 1],
             (dp_at(k), region))
        for k in range(1, dps)
    ]
    for copy in copies:
        copy.wait()
    part = half_sum[rows(dp * q, q)]
    for k in range(1, dps):
        part += from_dp[k - 1].astype(F32)
    quarter[...] = part
    to_z[...] = part.astype(BF16)
    copies = [
        send(to_z.at[rows(z_at(k) * s, s)], from_z.at[k - 1], s3.at[k - 1], r3.at[k - 1],
             (dp, 2 * z_at(k) + core))
        for k in range(1, zs)
    ]
    for copy in copies:
        copy.wait()
    part = quarter[rows(z * s, s)]
    for k in range(1, zs):
        part += from_z[k - 1].astype(F32)
    mine = core * h + dp * q
    whole[rows(mine + z * s, s)] = part.astype(BF16)

    def spread(start, n, ss, rs, targets):
        at = whole.at[rows(start, n)]
        copies = [send(at, at, ss.at[i], rs.at[i], to) for i, to in enumerate(targets)]
        for copy in copies:
            copy.wait()

    spread(mine + z * s, s, s4, r4, [(dp, 2 * z_at(k) + core) for k in range(1, zs)])
    spread(mine, q, s5, r5, [(dp_at(k), region) for k in range(1, dps)])
    spread(core * h, h, s6, r6, [mate])
    n = conv.shape[0]
    conv[...] = whole[:n].astype(F32)
    down[...] = whole[n : n + down.shape[0]].astype(F32)


def reduce_all(acc, c):
    dps, zs = lax.axis_size("dp"), lax.axis_size("region") // 2
    total = acc.shape[0]
    h = total // 2
    q = h // dps
    s = q // zs
    vmem = pl.BlockSpec(memory_space=pltpu.VMEM)
    sems = []
    for n in (1, dps - 1, zs - 1, zs - 1, dps - 1, 1):
        sems += [pltpu.SemaphoreType.DMA((n,))] * 2
    return pl.pallas_call(
        functools.partial(reduce_kernel, dps, zs),
        out_shape=(
            jax.ShapeDtypeStruct((27 * c, c), F32),
            jax.ShapeDtypeStruct((8 * c, c), F32),
        ),
        in_specs=[vmem],
        out_specs=(vmem, vmem),
        scratch_shapes=[
            pltpu.VMEM((h, c), F32),
            pltpu.VMEM((h, c), F32),
            pltpu.VMEM((h, c), BF16),
            pltpu.VMEM((dps - 1, q, c), BF16),
            pltpu.VMEM((q, c), F32),
            pltpu.VMEM((q, c), BF16),
            pltpu.VMEM((zs - 1, s, c), BF16),
            pltpu.VMEM((total, c), BF16),
        ] + sems,
        compiler_params=pltpu.CompilerParams(
            collective_id=0, has_side_effects=True, vmem_limit_bytes=32 * 1024 * 1024
        ),
    )(acc)


def octants(block, index):
    half = block.shape[0] // 2
    starts = (index // 4 * half, index // 2 % 2 * half, index % 2 * half, 0)
    return lax.dynamic_slice(block, starts, (half, half, half, block.shape[-1]))


def local(features, conv_weight, down_weight, coarse_cotangent, brick_coords, neighbours, parents):
    edge, c = features.shape[2], features.shape[-1]
    half = edge // 2
    region = lax.axis_index("region")
    peers = lax.axis_size("dp") * lax.axis_size("region")
    f = features.reshape(edge, edge, edge, c)
    cot = coarse_cotangent.reshape(edge, edge, edge, c)
    xyz = brick_coords.reshape(3)
    octant = xyz[0] % 2 * 4 + xyz[1] % 2 * 2 + xyz[2] % 2
    at_home = parents.reshape(()) == region

    other_cot = partner(cot, "region")
    flo = passed_along(f[edge - 1], "region", 1)
    fhi = passed_along(f[0], "region", -1)
    chosen = jnp.where(at_home, octants(cot, octant), octants(other_cot, octant))
    clo = passed_along(chosen[half - 1], "region", 1)
    chi = passed_along(chosen[0], "region", -1)

    unit = 16 * peers
    acc_rows = -(-35 * c // unit) * unit
    blocks, ig, acc = compute(
        neighbours.reshape(26), f, flo, fhi, chosen, clo, chi,
        conv_weight.reshape(27, c, c), down_weight.reshape(8, c, c), acc_rows,
    )
    conv_total, down_total = reduce_all(acc, c)

    tag = jnp.stack([parents.reshape(()), octant])
    other_blocks, other_tag = partner((blocks, tag), "region")
    own_at = jnp.where(at_home, octant, -1)
    other_at = jnp.where(other_tag[0] == region, other_tag[1], -1)
    grid = lambda axis: lax.broadcasted_iota(jnp.int32, (2, 1, 2, 1, 2, 1, 1), axis)
    number = grid(0) * 4 + grid(2) * 2 + grid(4)
    spread = lambda b: b.astype(F32).reshape(1, half, 1, half, 1, half, c)
    coarse = jnp.where(number == own_at, spread(blocks), 0.0) + jnp.where(
        number == other_at, spread(other_blocks), 0.0
    )
    return (
        coarse.astype(BF16).reshape(1, 1, edge, edge, edge, c),
        ig.reshape(1, 1, edge, edge, edge, c),
        conv_total.reshape(3, 3, 3, c, c),
        down_total.reshape(2, 2, 2, c, c),
    )


def solution(mesh):
    in_specs = (
        P("dp", "region", None, None, None, None),
        P(),
        P(),
        P("dp", "region", None, None, None, None),
        P("dp", "region", None),
        P("dp", "region", None),
        P("dp", "region"),
    )
    out_specs = (
        P("dp", "region", None, None, None, None),
        P("dp", "region", None, None, None, None),
        P(),
        P(),
    )
    return jax.shard_map(local, mesh=mesh, in_specs=in_specs, out_specs=out_specs, check_vma=False)
```

```python
import functools

import jax
import jax.numpy as jnp
from jax import lax
from jax.experimental import pallas as pl
from jax.experimental.pallas import tpu as pltpu
from jax.sharding import PartitionSpec as P

loss_scale = 1024.0
MESH = pl.DeviceIdType.MESH
F32, BF16 = jnp.float32, jnp.bfloat16


def nn(a, b):
    return lax.dot_general(a, b, (((1,), (0,)), ((), ())), preferred_element_type=F32)


def nt(a, b):
    return lax.dot_general(a, b, (((1,), (1,)), ((), ())), preferred_element_type=F32)


def shifted(s, low, mid, high):
    edge = s.shape[-2]
    axis = s.ndim - 2
    row = lax.broadcasted_iota(jnp.int32, s.shape, axis)
    first = pltpu.roll(s, 1, axis) * jnp.where(row == 0, low, mid)
    last = pltpu.roll(s, edge - 1, axis) * jnp.where(row == edge - 1, high, mid)
    return first, s * mid, last


def put_plane(dst, x, even, odd, low, mid, high):
    half, c = even.shape[0], even.shape[-1]
    for k, v in enumerate(shifted(even, low, mid, high)):
        dst[x, 0:half, :, 2 * k * c + c : 2 * k * c + 2 * c] = v.astype(BF16)
    for k, v in enumerate(shifted(odd, low, mid, high)):
        dst[x, 1 : half + 1, :, 2 * k * c : 2 * k * c + c] = v.astype(BF16)


def put_row(dst, x, y, row, low, mid, high):
    c = row.shape[-1]
    for k, v in enumerate(shifted(row, low, mid, high)):
        at = 2 * k * c + (y % 2) * c
        dst[x, y // 2, :, at : at + c] = v.astype(BF16)


def masks(nb, a):
    def m(b, c):
        i = (a + 1) * 9 + (b + 1) * 3 + (c + 1)
        i = i - 1 if i > 13 else i
        return jnp.where(nb[i] >= 0, 1.0, 0.0).astype(F32)

    return {b: (m(b, -1), m(b, 0), m(b, 1)) for b in (-1, 0, 1)}


def put_halo(dst, x, even, odd, mask):
    half, edge = even.shape[0], dst.shape[0]
    put_plane(dst, x, even, odd, *mask[0])
    put_row(dst, x, 0, odd[half - 1], *mask[-1])
    put_row(dst, x, edge - 1, even[0], *mask[1])


def zero_rows(dst, edge, c):
    z = jnp.zeros((edge, dst.shape[2], c), BF16)
    for k in range(3):
        dst[1 : edge + 1, 0, :, 2 * k * c : 2 * k * c + c] = z
        dst[1 : edge + 1, edge // 2, :, 2 * k * c + c : 2 * k * c + 2 * c] = z


def tap_of(s, pin, pout):
    b = 2 * s + pin - pout
    return b if 0 <= b <= 2 else None


class Reduction:
    def __init__(self, env, acc, whole, start, n, refs):
        self.env, self.acc, self.whole, self.start = env, acc, whole, start
        (self.to_core, self.from_core, self.to_dp, self.from_dp, self.to_z, self.from_z) = refs[:6]
        self.sems = refs[6:]
        self.h = n // 2
        self.q = self.h // env.dps
        self.s = self.q // env.zs
        self.half = self.start + env.core * self.h
        self.quarter = self.half + env.dp * self.q
        self.piece = self.quarter + env.z * self.s
        self.flying = []

    def go(self, stage, src, dst, peers):
        send, recv = self.sems[2 * stage], self.sems[2 * stage + 1]
        self.flying = [
            self.env.send(src(k), dst(k), send.at[k - 1], recv.at[k - 1], to)
            for k, to in enumerate(peers, 1)
        ]

    def land(self):
        for copy in self.flying:
            copy.wait()

    def spread(self, stage, at, n, peers):
        ref = self.whole.at[rows_at(at, n)]
        self.go(stage, lambda k: ref, lambda k: ref, peers)

    def step(self, stage):
        env, acc = self.env, self.acc
        h, q, s = self.h, self.q, self.s
        if stage > 0:
            self.land()
        if stage == 0:
            self.to_core[...] = acc[rows_at(self.start + (1 - env.core) * h, h)].astype(BF16)
            self.go(0, lambda k: self.to_core, lambda k: self.from_core, [env.mate])
        elif stage == 1:
            part = acc[rows_at(self.half, h)] + self.from_core[...].astype(F32)
            acc[rows_at(self.half, h)] = part
            self.to_dp[...] = part.astype(BF16)
            self.go(
                1,
                lambda k: self.to_dp.at[rows_at(env.dp_at(k) * q, q)],
                lambda k: self.from_dp.at[k - 1],
                env.dp_peers,
            )
        elif stage == 2:
            part = acc[rows_at(self.quarter, q)]
            for k in range(1, env.dps):
                part += self.from_dp[k - 1].astype(F32)
            acc[rows_at(self.quarter, q)] = part
            self.to_z[...] = part.astype(BF16)
            self.go(
                2,
                lambda k: self.to_z.at[rows_at(env.z_at(k) * s, s)],
                lambda k: self.from_z.at[k - 1],
                env.z_peers,
            )
        elif stage == 3:
            part = acc[rows_at(self.piece, s)]
            for k in range(1, env.zs):
                part += self.from_z[k - 1].astype(F32)
            self.whole[rows_at(self.piece, s)] = part.astype(BF16)
            self.spread(3, self.piece, s, env.z_peers)
        elif stage == 4:
            self.spread(4, self.quarter, q, env.dp_peers)
        elif stage == 5:
            self.spread(5, self.half, h, [env.mate])


def reduction_scratch(n, dps, zs, c):
    h = n // 2
    q = h // dps
    s = q // zs
    out = [
        pltpu.VMEM((h, c), BF16),
        pltpu.VMEM((h, c), BF16),
        pltpu.VMEM((h, c), BF16),
        pltpu.VMEM((dps - 1, q, c), BF16),
        pltpu.VMEM((q, c), BF16),
        pltpu.VMEM((zs - 1, s, c), BF16),
    ]
    for k in (1, dps - 1, zs - 1, zs - 1, dps - 1, 1):
        out += [pltpu.SemaphoreType.DMA((k,))] * 2
    return out


REDUCTION_REFS = 18


def rows_at(start, n):
    return pl.ds(pl.multiple_of(start, 16) if not isinstance(start, int) else start, n)


class Peers:
    def __init__(self, dps, zs):
        self.dps, self.zs = dps, zs
        n = 2 * zs
        self.dp, self.region = lax.axis_index("dp"), lax.axis_index("region")
        self.core, self.z = lax.rem(self.region, 2), lax.div(self.region, 2)
        self.mate = (self.dp, self.region + 1 - 2 * self.core)
        self.right = (self.dp, lax.rem(self.region + 1, n))
        self.left = (self.dp, lax.rem(self.region + n - 1, n))
        self.dp_peers = [(self.dp_at(k), self.region) for k in range(1, dps)]
        self.z_peers = [(self.dp, 2 * self.z_at(k) + self.core) for k in range(1, zs)]

    def dp_at(self, k):
        return lax.rem(self.dp + k, self.dps)

    def z_at(self, k):
        return lax.rem(self.z + k, self.zs)

    def enter(self):
        barrier = pltpu.get_barrier_semaphore()
        peers = [self.mate, self.right, self.left] + self.dp_peers + self.z_peers
        for peer in peers:
            pl.semaphore_signal(barrier, inc=1, device_id=peer, device_id_type=MESH)
        pl.semaphore_wait(barrier, len(peers))

    def send(self, src, dst, send, recv, to):
        copy = pltpu.make_async_remote_copy(
            src_ref=src, dst_ref=dst, send_sem=send, recv_sem=recv,
            device_id=to, device_id_type=MESH,
        )
        copy.start()
        return copy


def kernel(
    sizes, nb, own, f, cot, tag, cw, dw,
    coarse, ig, conv, down,
    field, wide, gfold, up, outf, gt, tt, acc, whole,
    flo, fhi, cot2, tag2, ch, clo, chi, blocks, blocks2, sends, recvs, *refs
):
    dps, zs, cut, conv_rows, down_rows = sizes
    env = Peers(dps, zs)
    edge, c = f.shape[0], f.shape[-1]
    half = edge // 2
    rows = half * edge
    n = REDUCTION_REFS
    first = Reduction(env, acc, whole, 0, cut, refs[:n])
    second = Reduction(env, acc, whole, cut, conv_rows - cut, refs[n : 2 * n])
    third = Reduction(env, acc, whole, conv_rows, down_rows, refs[2 * n :])

    def send(i, src, dst, to):
        return env.send(src, dst, sends.at[i], recvs.at[i], to)

    env.enter()
    cot_copy = send(0, cot, cot2, env.mate)
    tag_copy = send(1, tag, tag2, env.mate)
    up_copy = send(2, f.at[edge - 1], flo, env.right)
    down_copy = send(3, f.at[0], fhi, env.left)

    def window(x, m, a, s):
        return field[pl.ds(x + a, m), s : s + half].reshape(m * rows, 6 * c)

    def lhs(x, m):
        return jnp.concatenate([window(x, m, a, s) for a in range(3) for s in range(2)], -1)

    below, above = masks(nb, -1), masks(nb, 1)
    zero_rows(field, edge, c)

    @pl.loop(0, edge)
    def _(x):
        put_plane(field, x + 1, f[x, :, 0].astype(F32), f[x, :, 1].astype(F32), 0.0, 1.0, 0.0)

    zero = jnp.zeros((c, c), BF16)

    def weights(block):
        for a in range(3):
            for s in range(2):
                for k in range(3):
                    for pin in range(2):
                        at = ((2 * a + s) * 3 + k) * 2 * c + pin * c
                        for pout in range(2):
                            b = tap_of(s, pin, pout)
                            wide[at : at + c, pout * c : (pout + 1) * c] = (
                                zero if b is None else block(a, b, k)
                            )

    weights(lambda a, b, k: cw[9 * a + 3 * b + k])

    cot_copy.wait()
    tag_copy.wait()
    octant, home = own[1], own[0] == env.region
    picked = jnp.zeros((half, half, half, c), F32)
    for o in range(4):
        cut_of = (slice((o // 2) * half, (o // 2 + 1) * half), slice(o % 2 * half, (o % 2 + 1) * half))
        mine, theirs = cot[cut_of].astype(F32), cot2[cut_of].astype(F32)
        both = jnp.where(home, mine, theirs)
        for z in range(2):
            picked = jnp.where(
                octant == 2 * o + z, both[:, :, z * half : (z + 1) * half], picked
            )
    ch[...] = picked.astype(BF16)
    clo_copy = send(4, ch.at[half - 1], clo, env.right)
    chi_copy = send(5, ch.at[0], chi, env.left)

    up[...] = jnp.zeros_like(up)

    def lift(v):
        m = v.shape[0] * v.shape[1]
        v = v.astype(F32).reshape(m, half, c)
        for r in range(2):
            up[r, 0:m, pl.ds(r, half, 2), :] = v
        both = [up[r, 0:m].reshape(m * edge, c).astype(BF16) for r in range(2)]
        return jnp.concatenate(both, -1)

    def dwt(p):
        return jnp.concatenate(
            [jnp.concatenate([dw[4 * p + 2 * q + r] for r in range(2)], -1) for q in range(2)], 0
        )

    raised = lift(picked)
    for p in range(2):
        g = nt(raised, dwt(p)).astype(BF16).reshape(half, half, edge, 2 * c)
        for i in range(half):
            gfold[2 * i + p] = g[i]

    up_copy.wait()
    down_copy.wait()
    put_halo(field, 0, flo[:, 0].astype(F32), flo[:, 1].astype(F32), below)
    put_halo(field, edge + 1, fhi[:, 0].astype(F32), fhi[:, 1].astype(F32), above)

    flat = gfold[...].reshape(edge * rows, 2 * c)
    gt[...] = flat.astype(F32).T.astype(BF16)
    for a in range(3):
        for s in range(2):
            tt[s] = nn(gt[...], window(0, edge, a, s))
        for b in range(3):
            for k in range(3):
                total = jnp.zeros((c, c), F32)
                for s in range(2):
                    for pin in range(2):
                        for pout in range(2):
                            if tap_of(s, pin, pout) == b:
                                at = (2 * k + pin) * c
                                total += tt[s, pout * c : (pout + 1) * c, at : at + c]
                tap = 9 * a + 3 * b + k
                acc[tap * c : (tap + 1) * c] = total.T * (1.0 / loss_scale)
        if a == 1:
            first.step(0)
    if conv_rows > 27 * c:
        acc[27 * c : conv_rows] = jnp.zeros((conv_rows - 27 * c, c), F32)
    second.step(0)
    first.step(1)

    step = 4

    def forward(m, to):
        @pl.loop(m, to)
        def _(i):
            x = i * step
            out = nn(lhs(x, step), wide[...]).reshape(step, half, edge, 2 * c)
            for q in range(2):
                outf[q, pl.ds(x, step)] = (
                    (out[..., q * c : (q + 1) * c] + f[pl.ds(x, step), :, q].astype(F32))
                    .astype(BF16)
                    .astype(F32)
                )

    laps = edge // step
    forward(0, laps // 2)
    second.step(1)
    forward(laps // 2, laps)
    first.step(2)

    taken = []
    for p in range(2):
        for r in range(2):
            halves = []
            for q in range(2):
                parts = [
                    outf[q, 2 * i + p, :, pl.ds(r, half, 2), :].reshape(half * half, c)
                    for i in range(half)
                ]
                halves.append(jnp.concatenate(parts, 0).astype(BF16))
            taken.append(jnp.concatenate(halves, -1))
    dwf = jnp.concatenate(
        [dw[4 * p + 2 * q + r] for p in range(2) for r in range(2) for q in range(2)], 0
    )
    blocks[...] = nn(jnp.concatenate(taken, -1), dwf).astype(BF16).reshape(blocks.shape)
    blocks_copy = send(6, blocks, blocks2, env.mate)
    cht = ch[...].reshape(half**3, c).astype(F32).T.astype(BF16)
    for p in range(2):
        for r in range(2):
            d = nn(cht, taken[2 * p + r])
            for q in range(2):
                at = conv_rows + (4 * p + 2 * q + r) * c
                acc[at : at + c] = d[:, q * c : (q + 1) * c].T * (1.0 / loss_scale)
    if down_rows > 8 * c:
        acc[conv_rows + 8 * c :] = jnp.zeros((down_rows - 8 * c, c), F32)
    third.step(0)
    second.step(2)

    clo_copy.wait()
    chi_copy.wait()
    for edge_of, p, x, mask in ((clo, 1, 0, below), (chi, 0, edge + 1, above)):
        g = nt(lift(edge_of[...][None]), dwt(p)).astype(BF16).astype(F32)
        g = g.reshape(half, edge, 2 * c)
        put_halo(field, x, g[..., :c], g[..., c:], mask)

    @pl.loop(0, edge)
    def _(x):
        g = gfold[x].astype(F32)
        put_plane(field, x + 1, g[..., :c], g[..., c:], 0.0, 1.0, 0.0)

    third.step(1)
    first.step(3)
    weights(lambda a, b, k: cw[9 * (2 - a) + 3 * (2 - b) + 2 - k].T)
    second.step(3)

    def backward(m, to):
        @pl.loop(m, to)
        def _(i):
            x = i * step
            out = nn(lhs(x, step), wide[...]).reshape(step, half, edge, 2 * c)
            out = (out + gfold[pl.ds(x, step)].astype(F32)).astype(BF16)
            for q in range(2):
                ig[pl.ds(x, step), :, q] = out[..., q * c : (q + 1) * c]

    backward(0, laps // 2)
    first.step(4)
    third.step(2)
    second.step(4)
    backward(laps // 2, laps)
    third.step(3)
    first.step(5)

    blocks_copy.wait()
    mine, theirs = blocks[...].astype(F32), blocks2[...].astype(F32)
    own_tag, other_tag = tag[0:1, :], tag2[0:1, :]
    third.step(4)
    second.step(5)
    for o in range(4):
        parts = []
        for z in range(2):
            here = env.region * 8 + 2 * o + z
            ours = jnp.where(own_tag == here, 1.0, 0.0).astype(F32)
            others = jnp.where(other_tag == here, 1.0, 0.0).astype(F32)
            parts.append(mine * ours + theirs * others)
        x, y = o // 2 * half, o % 2 * half
        coarse[x : x + half, y : y + half] = jnp.concatenate(parts, 2).astype(BF16)
    third.step(5)
    first.land()
    conv[:cut] = whole[:cut].astype(F32)
    second.land()
    conv[cut:] = whole[cut : conv.shape[0]].astype(F32)
    third.land()
    down[...] = whole[conv_rows : conv_rows + down.shape[0]].astype(F32)


def local(features, conv_weight, down_weight, coarse_cotangent, brick_coords, neighbours, parents):
    edge, c = features.shape[2], features.shape[-1]
    half = edge // 2
    dps, regions = lax.axis_size("dp"), lax.axis_size("region")
    zs = regions // 2
    unit = 16 * dps * regions
    cut = 18 * c // unit * unit
    conv_rows = -(-27 * c // unit) * unit
    down_rows = -(-8 * c // unit) * unit
    xyz = brick_coords.reshape(3)
    octant = xyz[0] % 2 * 4 + xyz[1] % 2 * 2 + xyz[2] % 2
    parent = parents.reshape(())
    own = jnp.stack([parent, octant])
    tag = jnp.broadcast_to(parent * 8 + octant, (8, 128)).astype(jnp.int32)
    vmem = pl.BlockSpec(memory_space=pltpu.VMEM)
    smem = pl.BlockSpec(memory_space=pltpu.SMEM)
    plane = pltpu.VMEM((half, 2, edge, c), BF16)
    cube = pltpu.VMEM((half, half, half, c), BF16)
    layer = pltpu.VMEM((half, half, c), BF16)
    scratch = [
        pltpu.VMEM((edge + 2, half + 1, edge, 6 * c), BF16),
        pltpu.VMEM((36 * c, 2 * c), BF16),
        pltpu.VMEM((edge, half, edge, 2 * c), BF16),
        pltpu.VMEM((2, half * half, edge, c), F32),
        pltpu.VMEM((2, edge, half, edge, c), F32),
        pltpu.VMEM((2 * c, edge * half * edge), BF16),
        pltpu.VMEM((2, 2 * c, 6 * c), F32),
        pltpu.VMEM((conv_rows + down_rows, c), F32),
        pltpu.VMEM((conv_rows + down_rows, c), BF16),
        plane,
        plane,
        pltpu.VMEM((edge, edge, edge, c), BF16),
        pltpu.VMEM((8, 128), jnp.int32),
        cube,
        layer,
        layer,
        cube,
        cube,
        pltpu.SemaphoreType.DMA((7,)),
        pltpu.SemaphoreType.DMA((7,)),
    ]
    for n in (cut, conv_rows - cut, down_rows):
        scratch += reduction_scratch(n, dps, zs, c)
    coarse, ig, conv_total, down_total = pl.pallas_call(
        functools.partial(kernel, (dps, zs, cut, conv_rows, down_rows)),
        out_shape=(
            jax.ShapeDtypeStruct((edge, edge, edge, c), BF16),
            jax.ShapeDtypeStruct((edge, half, 2, edge, c), BF16),
            jax.ShapeDtypeStruct((27 * c, c), F32),
            jax.ShapeDtypeStruct((8 * c, c), F32),
        ),
        in_specs=[smem, smem] + [vmem] * 5,
        out_specs=(vmem,) * 4,
        scratch_shapes=scratch,
        compiler_params=pltpu.CompilerParams(
            collective_id=0, has_side_effects=True, vmem_limit_bytes=60 * 1024 * 1024
        ),
    )(
        neighbours.reshape(26), own, features.reshape(edge, half, 2, edge, c),
        coarse_cotangent.reshape(edge, edge, edge, c), tag,
        conv_weight.reshape(27, c, c), down_weight.reshape(8, c, c),
    )
    return (
        coarse.reshape(1, 1, edge, edge, edge, c),
        ig.reshape(1, 1, edge, edge, edge, c),
        conv_total.reshape(3, 3, 3, c, c),
        down_total.reshape(2, 2, 2, c, c),
    )


def solution(mesh):
    in_specs = (
        P("dp", "region", None, None, None, None),
        P(),
        P(),
        P("dp", "region", None, None, None, None),
        P("dp", "region", None),
        P("dp", "region", None),
        P("dp", "region"),
    )
    out_specs = (
        P("dp", "region", None, None, None, None),
        P("dp", "region", None, None, None, None),
        P(),
        P(),
    )
    return jax.shard_map(local, mesh=mesh, in_specs=in_specs, out_specs=out_specs, check_vma=False)
```

```python
import functools

import jax
import jax.numpy as jnp
from jax import lax
from jax.experimental import pallas as pl
from jax.experimental.pallas import tpu as pltpu
from jax.sharding import PartitionSpec as P

loss_scale = 1024.0
MESH = pl.DeviceIdType.MESH
F32, BF16 = jnp.float32, jnp.bfloat16


def nn(a, b):
    return lax.dot_general(a, b, (((1,), (0,)), ((), ())), preferred_element_type=F32)


def nt(a, b):
    return lax.dot_general(a, b, (((1,), (1,)), ((), ())), preferred_element_type=F32)


def shifted(s, low, mid, high):
    edge = s.shape[-2]
    axis = s.ndim - 2
    row = lax.broadcasted_iota(jnp.int32, s.shape, axis)
    first = pltpu.roll(s, 1, axis) * jnp.where(row == 0, low, mid)
    last = pltpu.roll(s, edge - 1, axis) * jnp.where(row == edge - 1, high, mid)
    return first, s * mid, last


def put_plane(dst, x, even, odd, low, mid, high):
    half, c = even.shape[0], even.shape[-1]
    for k, v in enumerate(shifted(even, low, mid, high)):
        dst[x, 0:half, :, 2 * k * c + c : 2 * k * c + 2 * c] = v.astype(BF16)
    for k, v in enumerate(shifted(odd, low, mid, high)):
        dst[x, 1 : half + 1, :, 2 * k * c : 2 * k * c + c] = v.astype(BF16)


def put_row(dst, x, y, row, low, mid, high):
    c = row.shape[-1]
    for k, v in enumerate(shifted(row, low, mid, high)):
        at = 2 * k * c + (y % 2) * c
        dst[x, y // 2, :, at : at + c] = v.astype(BF16)


def masks(nb, a):
    def m(b, c):
        i = (a + 1) * 9 + (b + 1) * 3 + (c + 1)
        i = i - 1 if i > 13 else i
        return jnp.where(nb[i] >= 0, 1.0, 0.0).astype(F32)

    return {b: (m(b, -1), m(b, 0), m(b, 1)) for b in (-1, 0, 1)}


def put_halo(dst, x, even, odd, mask):
    half, edge = even.shape[0], dst.shape[0]
    put_plane(dst, x, even, odd, *mask[0])
    put_row(dst, x, 0, odd[half - 1], *mask[-1])
    put_row(dst, x, edge - 1, even[0], *mask[1])


def zero_rows(dst, edge, c):
    z = jnp.zeros((edge, dst.shape[2], c), BF16)
    for k in range(3):
        dst[1 : edge + 1, 0, :, 2 * k * c : 2 * k * c + c] = z
        dst[1 : edge + 1, edge // 2, :, 2 * k * c + c : 2 * k * c + 2 * c] = z


def tap_of(s, pin, pout):
    b = 2 * s + pin - pout
    return b if 0 <= b <= 2 else None


class Reduction:
    def __init__(self, env, acc, whole, start, n, refs):
        self.env, self.acc, self.whole, self.start = env, acc, whole, start
        (self.to_core, self.from_core, self.to_dp, self.from_dp, self.to_z, self.from_z) = refs[:6]
        self.sems = refs[6:]
        self.h = n // 2
        self.q = self.h // env.dps
        self.s = self.q // env.zs
        self.half = self.start + env.core * self.h
        self.quarter = self.half + env.dp * self.q
        self.piece = self.quarter + env.z * self.s
        self.flying = []

    def go(self, stage, src, dst, peers):
        send, recv = self.sems[2 * stage], self.sems[2 * stage + 1]
        self.flying = [
            self.env.send(src(k), dst(k), send.at[k - 1], recv.at[k - 1], to)
            for k, to in enumerate(peers, 1)
        ]

    def land(self):
        for copy in self.flying:
            copy.wait()

    def spread(self, stage, at, n, peers):
        ref = self.whole.at[rows_at(at, n)]
        self.go(stage, lambda k: ref, lambda k: ref, peers)

    def step(self, stage):
        env, acc = self.env, self.acc
        h, q, s = self.h, self.q, self.s
        if stage > 0:
            self.land()
        if stage == 0:
            self.to_core[...] = acc[rows_at(self.start + (1 - env.core) * h, h)].astype(BF16)
            self.go(0, lambda k: self.to_core, lambda k: self.from_core, [env.mate])
        elif stage == 1:
            part = acc[rows_at(self.half, h)] + self.from_core[...].astype(F32)
            acc[rows_at(self.half, h)] = part
            self.to_dp[...] = part.astype(BF16)
            self.go(
                1,
                lambda k: self.to_dp.at[rows_at(env.dp_at(k) * q, q)],
                lambda k: self.from_dp.at[k - 1],
                env.dp_peers,
            )
        elif stage == 2:
            part = acc[rows_at(self.quarter, q)]
            for k in range(1, env.dps):
                part += self.from_dp[k - 1].astype(F32)
            acc[rows_at(self.quarter, q)] = part
            self.to_z[...] = part.astype(BF16)
            self.go(
                2,
                lambda k: self.to_z.at[rows_at(env.z_at(k) * s, s)],
                lambda k: self.from_z.at[k - 1],
                env.z_peers,
            )
        elif stage == 3:
            part = acc[rows_at(self.piece, s)]
            for k in range(1, env.zs):
                part += self.from_z[k - 1].astype(F32)
            self.whole[rows_at(self.piece, s)] = part.astype(BF16)
            self.spread(3, self.piece, s, env.z_peers)
        elif stage == 4:
            self.spread(4, self.quarter, q, env.dp_peers)
        elif stage == 5:
            self.spread(5, self.half, h, [env.mate])


def reduction_scratch(n, dps, zs, c):
    h = n // 2
    q = h // dps
    s = q // zs
    out = [
        pltpu.VMEM((h, c), BF16),
        pltpu.VMEM((h, c), BF16),
        pltpu.VMEM((h, c), BF16),
        pltpu.VMEM((dps - 1, q, c), BF16),
        pltpu.VMEM((q, c), BF16),
        pltpu.VMEM((zs - 1, s, c), BF16),
    ]
    for k in (1, dps - 1, zs - 1, zs - 1, dps - 1, 1):
        out += [pltpu.SemaphoreType.DMA((k,))] * 2
    return out


REDUCTION_REFS = 18


def rows_at(start, n):
    return pl.ds(pl.multiple_of(start, 16) if not isinstance(start, int) else start, n)


class Peers:
    def __init__(self, dps, zs):
        self.dps, self.zs = dps, zs
        n = 2 * zs
        self.dp, self.region = lax.axis_index("dp"), lax.axis_index("region")
        self.core, self.z = lax.rem(self.region, 2), lax.div(self.region, 2)
        self.mate = (self.dp, self.region + 1 - 2 * self.core)
        self.right = (self.dp, lax.rem(self.region + 1, n))
        self.left = (self.dp, lax.rem(self.region + n - 1, n))
        self.dp_peers = [(self.dp_at(k), self.region) for k in range(1, dps)]
        self.z_peers = [(self.dp, 2 * self.z_at(k) + self.core) for k in range(1, zs)]

    def dp_at(self, k):
        return lax.rem(self.dp + k, self.dps)

    def z_at(self, k):
        return lax.rem(self.z + k, self.zs)

    def enter(self):
        barrier = pltpu.get_barrier_semaphore()
        peers = [self.mate, self.right, self.left] + self.dp_peers + self.z_peers
        for peer in peers:
            pl.semaphore_signal(barrier, inc=1, device_id=peer, device_id_type=MESH)
        pl.semaphore_wait(barrier, len(peers))

    def send(self, src, dst, send, recv, to):
        copy = pltpu.make_async_remote_copy(
            src_ref=src, dst_ref=dst, send_sem=send, recv_sem=recv,
            device_id=to, device_id_type=MESH,
        )
        copy.start()
        return copy


def kernel(
    sizes, nb, xyz, parent, f, cot, cw, dw,
    coarse, ig, conv, down,
    field, wide, gfold, up, outf, gt, tt, acc, whole,
    flo, fhi, cot2, tag, tag2, ch, clo, chi, blocks, blocks2, sends, recvs, *refs
):
    dps, zs, cut, conv_rows, down_rows = sizes
    env = Peers(dps, zs)
    edge, c = f.shape[0], f.shape[-1]
    half = edge // 2
    rows = half * edge
    n = REDUCTION_REFS
    first = Reduction(env, acc, whole, 0, cut, refs[:n])
    second = Reduction(env, acc, whole, cut, conv_rows - cut, refs[n : 2 * n])
    third = Reduction(env, acc, whole, conv_rows, down_rows, refs[2 * n :])

    def send(i, src, dst, to):
        return env.send(src, dst, sends.at[i], recvs.at[i], to)

    octant = lax.rem(xyz[0], 2) * 4 + lax.rem(xyz[1], 2) * 2 + lax.rem(xyz[2], 2)
    tag[...] = jnp.full(tag.shape, parent[0] * 8 + octant, jnp.int32)
    env.enter()
    cot_copy = send(0, cot, cot2, env.mate)
    tag_copy = send(1, tag, tag2, env.mate)
    up_copy = send(2, f.at[edge - 1], flo, env.right)
    down_copy = send(3, f.at[0], fhi, env.left)

    def window(x, m, a, s):
        return field[pl.ds(x + a, m), s : s + half].reshape(m * rows, 6 * c)

    def lhs(x, m):
        return jnp.concatenate([window(x, m, a, s) for a in range(3) for s in range(2)], -1)

    below, above = masks(nb, -1), masks(nb, 1)
    zero_rows(field, edge, c)

    @pl.loop(0, edge)
    def _(x):
        put_plane(field, x + 1, f[x, :, 0].astype(F32), f[x, :, 1].astype(F32), 0.0, 1.0, 0.0)

    zero = jnp.zeros((c, c), BF16)

    def weights(block):
        for a in range(3):
            for s in range(2):
                for k in range(3):
                    for pin in range(2):
                        at = ((2 * a + s) * 3 + k) * 2 * c + pin * c
                        for pout in range(2):
                            b = tap_of(s, pin, pout)
                            wide[at : at + c, pout * c : (pout + 1) * c] = (
                                zero if b is None else block(a, b, k)
                            )

    weights(lambda a, b, k: cw[9 * a + 3 * b + k])

    cot_copy.wait()
    tag_copy.wait()
    home = parent[0] == env.region
    picked = jnp.zeros((half, half, half, c), F32)
    for o in range(4):
        cut_of = (slice((o // 2) * half, (o // 2 + 1) * half), slice(o % 2 * half, (o % 2 + 1) * half))
        mine, theirs = cot[cut_of].astype(F32), cot2[cut_of].astype(F32)
        both = jnp.where(home, mine, theirs)
        for z in range(2):
            picked = jnp.where(
                octant == 2 * o + z, both[:, :, z * half : (z + 1) * half], picked
            )
    ch[...] = picked.astype(BF16)
    clo_copy = send(4, ch.at[half - 1], clo, env.right)
    chi_copy = send(5, ch.at[0], chi, env.left)

    up[...] = jnp.zeros_like(up)

    def lift(v):
        m = v.shape[0] * v.shape[1]
        v = v.astype(F32).reshape(m, half, c)
        for r in range(2):
            up[r, 0:m, pl.ds(r, half, 2), :] = v
        both = [up[r, 0:m].reshape(m * edge, c).astype(BF16) for r in range(2)]
        return jnp.concatenate(both, -1)

    def dwt(p):
        return jnp.concatenate(
            [jnp.concatenate([dw[4 * p + 2 * q + r] for r in range(2)], -1) for q in range(2)], 0
        )

    raised = lift(picked)
    for p in range(2):
        g = nt(raised, dwt(p)).astype(BF16).reshape(half, half, edge, 2 * c)
        for i in range(half):
            gfold[2 * i + p] = g[i]

    up_copy.wait()
    down_copy.wait()
    put_halo(field, 0, flo[:, 0].astype(F32), flo[:, 1].astype(F32), below)
    put_halo(field, edge + 1, fhi[:, 0].astype(F32), fhi[:, 1].astype(F32), above)

    flat = gfold[...].reshape(edge * rows, 2 * c)
    gt[...] = flat.astype(F32).T.astype(BF16)
    for a in range(3):
        for s in range(2):
            tt[s] = nn(gt[...], window(0, edge, a, s))
        for b in range(3):
            for k in range(3):
                total = jnp.zeros((c, c), F32)
                for s in range(2):
                    for pin in range(2):
                        for pout in range(2):
                            if tap_of(s, pin, pout) == b:
                                at = (2 * k + pin) * c
                                total += tt[s, pout * c : (pout + 1) * c, at : at + c]
                tap = 9 * a + 3 * b + k
                acc[tap * c : (tap + 1) * c] = total.T * (1.0 / loss_scale)
        if a == 1:
            first.step(0)
    if conv_rows > 27 * c:
        acc[27 * c : conv_rows] = jnp.zeros((conv_rows - 27 * c, c), F32)
    second.step(0)
    first.step(1)

    step = 4

    def forward(m, to):
        @pl.loop(m, to)
        def _(i):
            x = i * step
            out = nn(lhs(x, step), wide[...]).reshape(step, half, edge, 2 * c)
            for q in range(2):
                outf[q, pl.ds(x, step)] = (
                    (out[..., q * c : (q + 1) * c] + f[pl.ds(x, step), :, q].astype(F32))
                    .astype(BF16)
                    .astype(F32)
                )

    laps = edge // step
    forward(0, laps // 2)
    second.step(1)
    forward(laps // 2, laps)
    first.step(2)

    taken = []
    for p in range(2):
        for r in range(2):
            halves = []
            for q in range(2):
                parts = [
                    outf[q, 2 * i + p, :, pl.ds(r, half, 2), :].reshape(half * half, c)
                    for i in range(half)
                ]
                halves.append(jnp.concatenate(parts, 0).astype(BF16))
            taken.append(jnp.concatenate(halves, -1))
    dwf = jnp.concatenate(
        [dw[4 * p + 2 * q + r] for p in range(2) for r in range(2) for q in range(2)], 0
    )
    blocks[...] = nn(jnp.concatenate(taken, -1), dwf).astype(BF16).reshape(blocks.shape)
    blocks_copy = send(6, blocks, blocks2, env.mate)
    cht = ch[...].reshape(half**3, c).astype(F32).T.astype(BF16)
    for p in range(2):
        for r in range(2):
            d = nn(cht, taken[2 * p + r])
            for q in range(2):
                at = conv_rows + (4 * p + 2 * q + r) * c
                acc[at : at + c] = d[:, q * c : (q + 1) * c].T * (1.0 / loss_scale)
    if down_rows > 8 * c:
        acc[conv_rows + 8 * c :] = jnp.zeros((down_rows - 8 * c, c), F32)
    third.step(0)
    second.step(2)

    clo_copy.wait()
    chi_copy.wait()
    for edge_of, p, x, mask in ((clo, 1, 0, below), (chi, 0, edge + 1, above)):
        g = nt(lift(edge_of[...][None]), dwt(p)).astype(BF16).astype(F32)
        g = g.reshape(half, edge, 2 * c)
        put_halo(field, x, g[..., :c], g[..., c:], mask)

    @pl.loop(0, edge)
    def _(x):
        g = gfold[x].astype(F32)
        put_plane(field, x + 1, g[..., :c], g[..., c:], 0.0, 1.0, 0.0)

    third.step(1)
    first.step(3)
    weights(lambda a, b, k: cw[9 * (2 - a) + 3 * (2 - b) + 2 - k].T)
    second.step(3)

    def backward(m, to):
        @pl.loop(m, to)
        def _(i):
            x = i * step
            out = nn(lhs(x, step), wide[...]).reshape(step, half, edge, 2 * c)
            out = (out + gfold[pl.ds(x, step)].astype(F32)).astype(BF16)
            for q in range(2):
                ig[pl.ds(x, step), :, q] = out[..., q * c : (q + 1) * c]

    quarter = laps // 4
    backward(0, quarter)
    third.step(2)
    first.step(4)
    backward(quarter, 2 * quarter)
    second.step(4)
    backward(2 * quarter, 3 * quarter)
    third.step(3)
    first.step(5)
    backward(3 * quarter, laps)
    third.step(4)
    second.step(5)

    blocks_copy.wait()
    mine, theirs = blocks[...].astype(F32), blocks2[...].astype(F32)
    own_tag, other_tag = tag[0:1, :], tag2[0:1, :]
    for o in range(4):
        parts = []
        for z in range(2):
            here = env.region * 8 + 2 * o + z
            ours = jnp.where(own_tag == here, 1.0, 0.0).astype(F32)
            others = jnp.where(other_tag == here, 1.0, 0.0).astype(F32)
            parts.append(mine * ours + theirs * others)
        x, y = o // 2 * half, o % 2 * half
        coarse[x : x + half, y : y + half] = jnp.concatenate(parts, 2).astype(BF16)
    third.step(5)
    first.land()
    conv[:cut] = whole[:cut].astype(F32)
    second.land()
    conv[cut:] = whole[cut : conv.shape[0]].astype(F32)
    third.land()
    down[...] = whole[conv_rows : conv_rows + down.shape[0]].astype(F32)


def local(features, conv_weight, down_weight, coarse_cotangent, brick_coords, neighbours, parents):
    edge, c = features.shape[2], features.shape[-1]
    half = edge // 2
    dps, regions = lax.axis_size("dp"), lax.axis_size("region")
    zs = regions // 2
    unit = 16 * dps * regions
    cut = 18 * c // unit * unit
    conv_rows = -(-27 * c // unit) * unit
    down_rows = -(-8 * c // unit) * unit
    vmem = pl.BlockSpec(memory_space=pltpu.VMEM)
    smem = pl.BlockSpec(memory_space=pltpu.SMEM)
    plane = pltpu.VMEM((half, 2, edge, c), BF16)
    cube = pltpu.VMEM((half, half, half, c), BF16)
    layer = pltpu.VMEM((half, half, c), BF16)
    scratch = [
        pltpu.VMEM((edge + 2, half + 1, edge, 6 * c), BF16),
        pltpu.VMEM((36 * c, 2 * c), BF16),
        pltpu.VMEM((edge, half, edge, 2 * c), BF16),
        pltpu.VMEM((2, half * half, edge, c), F32),
        pltpu.VMEM((2, edge, half, edge, c), F32),
        pltpu.VMEM((2 * c, edge * half * edge), BF16),
        pltpu.VMEM((2, 2 * c, 6 * c), F32),
        pltpu.VMEM((conv_rows + down_rows, c), F32),
        pltpu.VMEM((conv_rows + down_rows, c), BF16),
        plane,
        plane,
        pltpu.VMEM((edge, edge, edge, c), BF16),
        pltpu.VMEM((8, 128), jnp.int32),
        pltpu.VMEM((8, 128), jnp.int32),
        cube,
        layer,
        layer,
        cube,
        cube,
        pltpu.SemaphoreType.DMA((7,)),
        pltpu.SemaphoreType.DMA((7,)),
    ]
    for n in (cut, conv_rows - cut, down_rows):
        scratch += reduction_scratch(n, dps, zs, c)
    coarse, ig, conv_total, down_total = pl.pallas_call(
        functools.partial(kernel, (dps, zs, cut, conv_rows, down_rows)),
        out_shape=(
            jax.ShapeDtypeStruct((edge, edge, edge, c), BF16),
            jax.ShapeDtypeStruct((edge, half, 2, edge, c), BF16),
            jax.ShapeDtypeStruct((27 * c, c), F32),
            jax.ShapeDtypeStruct((8 * c, c), F32),
        ),
        in_specs=[smem] * 3 + [vmem] * 4,
        out_specs=(vmem,) * 4,
        scratch_shapes=scratch,
        compiler_params=pltpu.CompilerParams(
            collective_id=0, has_side_effects=True, vmem_limit_bytes=60 * 1024 * 1024
        ),
    )(
        neighbours.reshape(26), brick_coords.reshape(3), parents.reshape(1),
        features.reshape(edge, half, 2, edge, c), coarse_cotangent.reshape(edge, edge, edge, c),
        conv_weight.reshape(27, c, c), down_weight.reshape(8, c, c),
    )
    return (
        coarse.reshape(1, 1, edge, edge, edge, c),
        ig.reshape(1, 1, edge, edge, edge, c),
        conv_total.reshape(3, 3, 3, c, c),
        down_total.reshape(2, 2, 2, c, c),
    )


def solution(mesh):
    in_specs = (
        P("dp", "region", None, None, None, None),
        P(),
        P(),
        P("dp", "region", None, None, None, None),
        P("dp", "region", None),
        P("dp", "region", None),
        P("dp", "region"),
    )
    out_specs = (
        P("dp", "region", None, None, None, None),
        P("dp", "region", None, None, None, None),
        P(),
        P(),
    )
    return jax.shard_map(local, mesh=mesh, in_specs=in_specs, out_specs=out_specs, check_vma=False)
```
